32 devices in a mesh: dp: 32 (over z, y, x, core).
Axes of the slice: x: 2, y: 2, z: 4, core: 2. Of those that a mesh axis runs over, the one named last changes fastest.
Arguments:
- inputs: bfloat16 [4096, 1024], P('dp'), may hold values from -6 to 6
- segment_ids: int32 [32, 128], P('dp'), may hold values from 0 to 3, never falling along the last dimension, each value on 1 to 64 neighbouring positions
- cotangent: bfloat16 [4096, 1024], P('dp'), may hold values from -6 to 6
- w_qkv: bfloat16 [1024, 3072], P('dp'), may hold values from -2 to 2
- bias_q: bfloat16 [1024], P('dp'), may hold values from -3 to 3
- bias_v: bfloat16 [1024], P('dp'), may hold values from -3 to 3
- w_out: bfloat16 [1024, 1024], P('dp'), may hold values from -0.5 to 0.5
- bias_out: bfloat16 [1024], P('dp'), may hold values from -3 to 3
- gain_one: bfloat16 [1024], P('dp'), may hold values from 0.5 to 1.5
- shift_one: bfloat16 [1024], P('dp'), may hold values from -3 to 3
- w_up: bfloat16 [1024, 4096], P('dp'), may hold values from -0.1875 to 0.1875
- bias_up: bfloat16 [4096], P('dp'), may hold values from -3 to 3
- w_down: bfloat16 [4096, 1024], P('dp'), may hold values from -0.125 to 0.125
- bias_down: bfloat16 [1024], P('dp'), may hold values from -3 to 3
- gain_two: bfloat16 [1024], P('dp'), may hold values from 0.5 to 1.5
- shift_two: bfloat16 [1024], P('dp'), may hold values from -3 to 3
Outputs:
- output: bfloat16 [4096, 1024], P('dp')
- grad_input: float32 [4096, 1024], P('dp')
- grad_w_qkv: float32 [1024, 3072], P('dp')
- grad_w_out: float32 [1024, 1024], P('dp')
- grad_w_up: float32 [1024, 4096], P('dp')
- grad_w_down: float32 [4096, 1024], P('dp')
- grad_bias_q: float32 [1024], P('dp')
- grad_bias_v: float32 [1024], P('dp')
- grad_bias_out: float32 [1024], P('dp')
- grad_gain_one: float32 [1024], P('dp')
- grad_shift_one: float32 [1024], P('dp')
- grad_bias_up: float32 [4096], P('dp')
- grad_bias_down: float32 [1024], P('dp')
- grad_gain_two: float32 [1024], P('dp')
- grad_shift_two: float32 [1024], P('dp')
The draws below stay inside these ranges and needn't reach their ends.
Inputs may be any that keep to these rules, and one draw needn't show every extreme that they name: `segment_ids`: numbers never fall along a row; each row holds 4 sequences.
All inputs are finite; a program needn't handle non-finite values.
Results may differ from the reference program's by a relative error of at most 0.014.
The reference program's roundings to bfloat16 on the way count: a program that leaves them out, or rounds other values in their place, can miss the bound.
Values may be sent and summed in bfloat16 or wider, within the bound.
A program may use at most 192 MiB of HBM per device.

```python
import math
import jax
import jax.numpy as jnp
import numpy as np
from jax import lax

HEADS = 16
HEAD_DIM = 64
D = 1024
FF = 4096
TOK_DEV = 128
MAXLEN = 64
SEQ_DEV = 4
TOKENS = 4096
N_DP = 32


def draw_w_qkv(key, part):
    base = jax.random.truncated_normal(key, -6.0, 6.0, (D, 3 * D), jnp.float32) * D ** (-0.5)
    return base.astype(jnp.bfloat16)


def spiked(drawn, rng, source, target, blocks, factor):
    def block_of(dim):
        return (jnp.arange(drawn.shape[dim]) // (drawn.shape[dim] // blocks)).reshape((-1,) + (1,) * (drawn.ndim - 1 - dim))

    one_side = jax.random.permutation(rng, blocks)[block_of(target)]
    second = (block_of(target) + blocks // 2) % blocks
    return jnp.where((block_of(source) == one_side) | (block_of(source) == second), factor * drawn, drawn)


def block_levels(key, dims, split, least, high):
    level, own = 1.0, jax.random.fold_in(key, 6)
    for dim, parts in split:
        heights = jnp.exp(jax.random.uniform(jax.random.fold_in(own, dim), (parts,), jnp.float32, least / len(split), high / len(split)))
        level = level * jnp.repeat(heights, dims[dim] // parts).reshape([-1 if axis == dim else 1 for axis in range(len(dims))])
    return level


def split_up(count, total, reach, skew):
    portions = [(1 << 20) // math.isqrt(standing ** skew) + 1 for standing in range(2, count + 1)]
    surplus, holding = total - reach - (count - 1), [1] * (count - 1)
    while surplus > 0:
        movable = [i for i in range(count - 1) if holding[i] < reach]
        whole, left = sum([portions[i] for i in movable]), surplus
        for i in movable:
            addition = min(reach - holding[i], max(1, left * portions[i] // whole), surplus)
            holding[i] = holding[i] + addition
            surplus = surplus - addition
    return np.array([reach] + holding)


def ragged_sizes(stream_key, count, total, reach, lean):
    if count == 2:
        one = jax.random.randint(stream_key, (), max(1, total - reach), min(reach, total - 1) + 1)
        return jnp.stack([one, total - one])
    lengths = jnp.asarray(split_up(count, total, reach, lean), jnp.int32)
    couples = (count - 1) // 2
    donor, taker = lengths[1:1 + 2 * couples:2], lengths[2:2 + 2 * couples:2]
    margin = jnp.minimum(donor - 1, reach - taker)
    moved = jax.random.randint(jax.random.fold_in(stream_key, 1), (couples,), 0, 1 << 20) % (margin + 1)
    lengths = lengths.at[1:1 + 2 * couples:2].set(donor - moved).at[2:2 + 2 * couples:2].set(taker + moved)
    return lengths[jax.random.permutation(jax.random.fold_in(stream_key, 2), count)]


def noise(stream_key, extent, spread, bound, pieces=(), kind=jnp.bfloat16):
    factor_of = block_levels(stream_key, extent, pieces, -0.22, 0.18) if pieces else 1.0
    values = jax.random.normal(stream_key, extent, jnp.float32) * spread * factor_of
    return jnp.minimum(jnp.maximum(values, -bound), bound).astype(kind)


def gaussian_with(own_key, extent, width, most, pieces, heavy, dtype=jnp.bfloat16):
    drawn = width * jax.random.normal(own_key, extent, jnp.float32)
    if pieces:
        drawn = drawn * block_levels(own_key, extent, pieces, -0.22, 0.18)
    return jnp.clip(spiked(drawn, jax.random.fold_in(own_key, 3), *heavy), -most, most).astype(dtype)


def setup_inputs(seed: int = 0) -> dict:
    key_of = jax.random.split(jax.random.key(seed), 17)
    return {
        "inputs": noise(key_of[0], (TOKENS, D), 1.0, 6.0, ((0, 32),)),
        "segment_ids": jax.vmap(lambda own: jnp.searchsorted(jnp.cumsum(ragged_sizes(own, SEQ_DEV, TOK_DEV, MAXLEN, 2)), jnp.arange(TOK_DEV), side="right"))(jax.random.split(key_of[1], N_DP)).reshape((N_DP, TOK_DEV)).astype(jnp.int32),
        "cotangent": gaussian_with(key_of[2], (TOKENS, D), 1.0, 6.0, ((0, 32),), (0, 1, 32, 2.75)),
        "w_qkv": draw_w_qkv(jax.random.fold_in(key_of[16], 71), 0),
        "bias_q": noise(key_of[4], (D,), 0.5, 3.0, ((0, 32),)),
        "bias_v": noise(key_of[5], (D,), 0.5, 3.0, ((0, 32),)),
        "w_out": noise(key_of[6], (D, D), (D // 8) ** -0.5, 0.5, ((0, 32),)),
        "bias_out": noise(key_of[7], (D,), 0.5, 3.0, ((0, 32),)),
        "gain_one": jnp.clip(1.0 + 0.1 * jax.random.normal(key_of[8], (D,), jnp.float32), 0.5, 1.5).astype(jnp.bfloat16),
        "shift_one": noise(key_of[9], (D,), 0.5, 3.0, ((0, 32),)),
        "w_up": noise(key_of[10], (D, FF), D ** -0.5, 0.1875, ((0, 32),)),
        "bias_up": noise(key_of[11], (FF,), 0.5, 3.0, ((0, 32),)),
        "w_down": noise(key_of[12], (FF, D), (FF // 2) ** -0.5, 0.125, ((0, 32),)),
        "bias_down": noise(key_of[13], (D,), 0.5, 3.0, ((0, 32),)),
        "gain_two": jnp.clip(1.0 + 0.1 * jax.random.normal(key_of[14], (D,), jnp.float32), 0.5, 1.5).astype(jnp.bfloat16),
        "shift_two": noise(key_of[15], (D,), 0.5, 3.0, ((0, 32),)),
    }


EPS = 1e-06
ROOT_HALF = 0.7071067811865476
INV_ROOT_TWO_PI = 0.3989422804014327

def layer_norm(hidden, gain, shift):
    centred = hidden - lax.optimization_barrier(jnp.mean(hidden, axis=-1, keepdims=True))
    rstd = lax.rsqrt(lax.optimization_barrier(jnp.mean(centred * centred, axis=-1, keepdims=True)) + EPS)
    normed = centred * rstd
    return (normed * gain.astype(jnp.float32) + shift.astype(jnp.float32), normed, rstd)

def norm_back(grad_y, normed, rstd, gain):
    grad_n = grad_y * gain.astype(jnp.float32)
    return rstd * (grad_n - lax.optimization_barrier(jnp.mean(grad_n, axis=-1, keepdims=True)) - normed * lax.optimization_barrier(jnp.mean(grad_n * normed, axis=-1, keepdims=True)))

def scores_of(query, keys, segs):
    raw = jnp.einsum('qhd,khd->hqk', query.astype(jnp.float32), keys.astype(jnp.float32)) * 0.125
    allowed = segs[:, None] == segs[None, :]
    return jnp.where(allowed[None], raw, -1e+30)

def block_pass(inputs, segs, cotangent, w_qkv, bias_q, bias_v, w_out, bias_out, gain_one, shift_one, w_up, bias_up, w_down, bias_down, gain_two, shift_two):
    count = inputs.shape[0]
    zeros = jnp.zeros((D,), jnp.float32)
    qkv_bias = jnp.concatenate([bias_q.astype(jnp.float32), zeros, bias_v.astype(jnp.float32)])
    qkv = (jnp.dot(inputs, w_qkv, preferred_element_type=jnp.float32) + qkv_bias).astype(jnp.bfloat16)
    query = qkv[:, :D].reshape(count, HEADS, HEAD_DIM)
    keys = qkv[:, D:2 * D].reshape(count, HEADS, HEAD_DIM)
    values = qkv[:, 2 * D:].reshape(count, HEADS, HEAD_DIM)
    scores = scores_of(query, keys, segs)
    peak = lax.optimization_barrier(jnp.max(scores, axis=-1, keepdims=True))
    lse = peak + jnp.log(lax.optimization_barrier(jnp.sum(jnp.exp(scores - peak), axis=-1, keepdims=True)))
    probs = jnp.exp(scores - lse)
    probs_b = probs.astype(jnp.bfloat16)
    ctx = jnp.einsum('hqk,khd->qhd', probs_b.astype(jnp.float32), values.astype(jnp.float32)).astype(jnp.bfloat16)
    ctx_flat = ctx.reshape(count, D)
    hidden_one = inputs.astype(jnp.float32) + jnp.dot(ctx_flat, w_out, preferred_element_type=jnp.float32) + bias_out.astype(jnp.float32)
    first, normed_one, rstd_one = layer_norm(hidden_one, gain_one, shift_one)
    first_b = first.astype(jnp.bfloat16)
    upper = jnp.dot(first_b, w_up, preferred_element_type=jnp.float32) + bias_up.astype(jnp.float32)
    erf_part = jax.scipy.special.erf(upper * ROOT_HALF)
    act = (0.5 * upper * (1.0 + erf_part)).astype(jnp.bfloat16)
    hidden_two = first_b.astype(jnp.float32) + jnp.dot(act, w_down, preferred_element_type=jnp.float32) + bias_down.astype(jnp.float32)
    final, normed_two, rstd_two = layer_norm(hidden_two, gain_two, shift_two)
    output = final.astype(jnp.bfloat16)
    grad_out = cotangent.astype(jnp.float32)
    g_gain_two = lax.optimization_barrier(jnp.sum(grad_out * normed_two, axis=0))
    g_shift_two = lax.optimization_barrier(jnp.sum(grad_out, axis=0))
    grad_h2 = norm_back(grad_out, normed_two, rstd_two, gain_two)
    grad_m = grad_h2.astype(jnp.bfloat16)
    g_w_down = jnp.dot(act.T, grad_m, preferred_element_type=jnp.float32)
    g_bias_down = lax.optimization_barrier(jnp.sum(grad_h2, axis=0))
    slope = 0.5 * (1.0 + erf_part) + upper * jnp.exp(-0.5 * upper * upper) * INV_ROOT_TWO_PI
    grad_u = jnp.dot(grad_m, w_down.T, preferred_element_type=jnp.float32) * slope
    grad_u_b = grad_u.astype(jnp.bfloat16)
    g_w_up = jnp.dot(first_b.T, grad_u_b, preferred_element_type=jnp.float32)
    g_bias_up = lax.optimization_barrier(jnp.sum(grad_u, axis=0))
    grad_y1 = grad_h2 + jnp.dot(grad_u_b, w_up.T, preferred_element_type=jnp.float32)
    g_gain_one = lax.optimization_barrier(jnp.sum(grad_y1 * normed_one, axis=0))
    g_shift_one = lax.optimization_barrier(jnp.sum(grad_y1, axis=0))
    grad_h1 = norm_back(grad_y1, normed_one, rstd_one, gain_one)
    grad_a = grad_h1.astype(jnp.bfloat16)
    g_w_out = jnp.dot(ctx_flat.T, grad_a, preferred_element_type=jnp.float32)
    g_bias_out = lax.optimization_barrier(jnp.sum(grad_h1, axis=0))
    grad_ctx = jnp.dot(grad_a, w_out.T, preferred_element_type=jnp.float32).astype(jnp.bfloat16).reshape(count, HEADS, HEAD_DIM)
    again = jnp.exp(scores_of(query, keys, segs) - lse)
    again_b = again.astype(jnp.bfloat16)
    delta = lax.optimization_barrier(jnp.sum(grad_ctx.astype(jnp.float32) * ctx.astype(jnp.float32), axis=-1)).T
    grad_p = jnp.einsum('qhd,khd->hqk', grad_ctx.astype(jnp.float32), values.astype(jnp.float32))
    grad_s = (again * (grad_p - delta[:, :, None]) * 0.125).astype(jnp.bfloat16).astype(jnp.float32)
    grad_q = jnp.einsum('hqk,khd->qhd', grad_s, keys.astype(jnp.float32)).reshape(count, D)
    grad_k = jnp.einsum('hqk,qhd->khd', grad_s, query.astype(jnp.float32)).reshape(count, D)
    grad_v = jnp.einsum('hqk,qhd->khd', again_b.astype(jnp.float32), grad_ctx.astype(jnp.float32)).reshape(count, D)
    g_bias_q = lax.optimization_barrier(jnp.sum(grad_q, axis=0))
    g_bias_v = lax.optimization_barrier(jnp.sum(grad_v, axis=0))
    grad_qkv = jnp.concatenate([grad_q, grad_k, grad_v], axis=1).astype(jnp.bfloat16)
    g_w_qkv = jnp.dot(inputs.T, grad_qkv, preferred_element_type=jnp.float32)
    grad_in = jnp.dot(grad_qkv, w_qkv.T, preferred_element_type=jnp.float32) + grad_h1
    grads = (g_w_qkv, g_w_out, g_w_up, g_w_down, g_bias_q, g_bias_v, g_bias_out, g_gain_one, g_shift_one, g_bias_up, g_bias_down, g_gain_two, g_shift_two)
    return (output, grad_in, grads)

def reference(inputs, segment_ids, cotangent, w_qkv, bias_q, bias_v, w_out, bias_out, gain_one, shift_one, w_up, bias_up, w_down, bias_down, gain_two, shift_two):
    params = (w_qkv, bias_q, bias_v, w_out, bias_out, gain_one, shift_one, w_up, bias_up, w_down, bias_down, gain_two, shift_two)
    rows_in = inputs.reshape(N_DP, TOK_DEV, D)
    rows_cot = cotangent.reshape(N_DP, TOK_DEV, D)
    start = (jnp.zeros((D, 3 * D), jnp.float32), jnp.zeros((D, D), jnp.float32), jnp.zeros((D, FF), jnp.float32), jnp.zeros((FF, D), jnp.float32), jnp.zeros((D,), jnp.float32), jnp.zeros((D,), jnp.float32), jnp.zeros((D,), jnp.float32), jnp.zeros((D,), jnp.float32), jnp.zeros((D,), jnp.float32), jnp.zeros((FF,), jnp.float32), jnp.zeros((D,), jnp.float32), jnp.zeros((D,), jnp.float32), jnp.zeros((D,), jnp.float32))

    def step(carry, item):
        block_in, segs, block_cot = item
        output, grad_in, grads = block_pass(block_in, segs, block_cot, *params)
        return (jax.tree.map(lambda a, b: a + b, carry, grads), (output, grad_in))
    totals, (outputs, grad_inputs) = lax.scan(step, start, (rows_in, segment_ids, rows_cot))
    return (outputs.reshape(TOKENS, D), grad_inputs.reshape(TOKENS, D), totals[0], totals[1], totals[2], totals[3], totals[4], totals[5], totals[6], totals[7], totals[8], totals[9], totals[10], totals[11], totals[12])
```

```python
import functools

import jax
import jax.numpy as jnp
from jax import lax
from jax.sharding import PartitionSpec as P

HEAD_DIM = 64


EPS = 1e-06
ROOT_HALF = 0.7071067811865476
INV_ROOT_TWO_PI = 0.3989422804014327


def layer_norm(hidden, gain, shift):
    centred = hidden - jnp.mean(hidden, axis=-1, keepdims=True)
    rstd = lax.rsqrt(jnp.mean(centred * centred, axis=-1, keepdims=True) + EPS)
    normed = centred * rstd
    return (normed * gain.astype(jnp.float32) + shift.astype(jnp.float32), normed, rstd)


def norm_back(grad_y, normed, rstd, gain):
    grad_n = grad_y * gain.astype(jnp.float32)
    return rstd * (
        grad_n
        - jnp.mean(grad_n, axis=-1, keepdims=True)
        - normed * jnp.mean(grad_n * normed, axis=-1, keepdims=True)
    )


def scores_of(query, keys, segs):
    raw = jnp.einsum("qhd,khd->hqk", query, keys, preferred_element_type=jnp.float32) * 0.125
    allowed = segs[:, None] == segs[None, :]
    return jnp.where(allowed[None], raw, -1e30)


def times_transposed(left, right):
    return lax.dot_general(
        left, right, (((1,), (1,)), ((), ())), preferred_element_type=jnp.float32
    )


def transposed_times(left, right):
    return lax.dot_general(
        left, right, (((0,), (0,)), ((), ())), preferred_element_type=jnp.float32
    )


def axes_bits(shards):
    chips = shards.bit_length() - 2
    low = chips // 3
    x_bits = tuple(range(1, 1 + low))
    y_bits = tuple(range(1 + low, 1 + 2 * low))
    z_bits = tuple(range(1 + 2 * low, 1 + chips))
    return x_bits, y_bits, z_bits


def halving_order(shards, swapped=False):
    x_bits, y_bits, z_bits = axes_bits(shards)
    plane = y_bits + x_bits if swapped else x_bits + y_bits
    return (0,) + plane + z_bits


def trade(value, bit, shards):
    pairs = [(i, i ^ (1 << bit)) for i in range(shards)]
    return lax.ppermute(value, "dp", pairs)


def my_bit(bit):
    return (lax.axis_index("dp") >> bit) & 1


def gather(shard, order, shards):
    have = shard
    joined = []
    for bit in order:
        other = trade(have, bit, shards)
        axis = sum(1 for b in joined if b > bit)
        upper = my_bit(bit) == 1
        have = jnp.stack(
            [jnp.where(upper, other, have), jnp.where(upper, have, other)], axis=axis
        )
        joined.append(bit)
    return have


def scatter(value, order, shards, first_type):
    left = sorted(order, reverse=True)
    value = value.reshape((2,) * len(left) + value.shape[1:])
    for step, bit in enumerate(order):
        axis = left.index(bit)
        mine = my_bit(bit)
        keep = lax.dynamic_index_in_dim(value, mine, axis, keepdims=False)
        give = lax.dynamic_index_in_dim(value, 1 - mine, axis, keepdims=False)
        kind = first_type if step == 0 else jnp.float32
        value = keep + trade(give.astype(kind), bit, shards).astype(jnp.float32)
        left.remove(bit)
    return value


def gather_rows(shard, shards):
    half = shard.shape[0] // 2
    parts = []
    for i in range(2):
        order = tuple(reversed(halving_order(shards, bool(i))))
        parts.append(gather(shard[i * half : (i + 1) * half], order, shards))
    k = parts[0].ndim - 2
    return jnp.concatenate(parts, axis=k).reshape(-1, shard.shape[1])


def pair_sum(left, right, shards):
    tokens = left.shape[0]
    rows = left.shape[1] // shards
    split = left.reshape(tokens, shards // 2, 2, rows)
    core = my_bit(0)
    keep = lax.dynamic_index_in_dim(split, core, 2, keepdims=False).reshape(tokens, -1)
    give = lax.dynamic_index_in_dim(split, 1 - core, 2, keepdims=False).reshape(tokens, -1)
    both_left = jnp.concatenate([keep, trade(give, 0, shards)], axis=0)
    both_right = jnp.concatenate([right, trade(right, 0, shards)], axis=0)
    total = transposed_times(both_left, both_right).reshape(shards // 2, rows, -1)
    half = rows // 2
    parts = []
    for i in range(2):
        order = halving_order(shards, bool(i))[1:]
        parts.append(scatter(total[:, i * half : (i + 1) * half], order, shards, jnp.bfloat16))
    return jnp.concatenate(parts, axis=0)


def per_device(
    shards,
    inputs,
    segment_ids,
    cotangent,
    w_qkv,
    bias_q,
    bias_v,
    w_out,
    bias_out,
    gain_one,
    shift_one,
    w_up,
    bias_up,
    w_down,
    bias_down,
    gain_two,
    shift_two,
):
    count = inputs.shape[0]
    width = inputs.shape[1]
    heads = width // HEAD_DIM
    segs = segment_ids[0]
    f_qkv = gather_rows(w_qkv, shards)
    f_out = gather_rows(w_out, shards)
    f_up = gather_rows(w_up, shards)
    f_down = gather_rows(w_down, shards)
    vecs = (bias_q, bias_v, bias_out, gain_one, shift_one, bias_up, bias_down, gain_two, shift_two)
    every = gather(
        jnp.concatenate(vecs)[None], tuple(reversed(halving_order(shards))), shards
    ).reshape(shards, -1)
    wide = []
    at = 0
    for v in vecs:
        wide.append(every[:, at : at + v.shape[0]].reshape(-1))
        at += v.shape[0]
    f_bq, f_bv, f_bo, f_g1, f_s1, f_bu, f_bd, f_g2, f_s2 = wide
    zeros = jnp.zeros((width,), jnp.float32)
    qkv_bias = jnp.concatenate([f_bq.astype(jnp.float32), zeros, f_bv.astype(jnp.float32)])
    qkv = (jnp.dot(inputs, f_qkv, preferred_element_type=jnp.float32) + qkv_bias).astype(
        jnp.bfloat16
    )
    query = qkv[:, :width].reshape(count, heads, HEAD_DIM)
    keys = qkv[:, width : 2 * width].reshape(count, heads, HEAD_DIM)
    values = qkv[:, 2 * width :].reshape(count, heads, HEAD_DIM)
    scores = scores_of(query, keys, segs)
    peak = jnp.max(scores, axis=-1, keepdims=True)
    lse = peak + jnp.log(jnp.sum(jnp.exp(scores - peak), axis=-1, keepdims=True))
    probs_b = jnp.exp(scores - lse).astype(jnp.bfloat16)
    ctx = jnp.einsum("hqk,khd->qhd", probs_b, values, preferred_element_type=jnp.float32).astype(
        jnp.bfloat16
    )
    ctx_flat = ctx.reshape(count, width)
    hidden_one = (
        inputs.astype(jnp.float32)
        + jnp.dot(ctx_flat, f_out, preferred_element_type=jnp.float32)
        + f_bo.astype(jnp.float32)
    )
    first, normed_one, rstd_one = layer_norm(hidden_one, f_g1, f_s1)
    first_b = first.astype(jnp.bfloat16)
    upper = jnp.dot(first_b, f_up, preferred_element_type=jnp.float32) + f_bu.astype(jnp.float32)
    erf_part = jax.scipy.special.erf(upper * ROOT_HALF)
    act = (0.5 * upper * (1.0 + erf_part)).astype(jnp.bfloat16)
    hidden_two = (
        first_b.astype(jnp.float32)
        + jnp.dot(act, f_down, preferred_element_type=jnp.float32)
        + f_bd.astype(jnp.float32)
    )
    final, normed_two, rstd_two = layer_norm(hidden_two, f_g2, f_s2)
    output = final.astype(jnp.bfloat16)
    b_qkv, b_out, b_up, b_down, b_g1, b_g2 = f_qkv, f_out, f_up, f_down, f_g1, f_g2
    grad_out = cotangent.astype(jnp.float32)
    g_gain_two = jnp.sum(grad_out * normed_two, axis=0)
    g_shift_two = jnp.sum(grad_out, axis=0)
    grad_h2 = norm_back(grad_out, normed_two, rstd_two, b_g2)
    grad_m = grad_h2.astype(jnp.bfloat16)
    g_w_down = pair_sum(act, grad_m, shards)
    g_bias_down = jnp.sum(grad_h2, axis=0)
    slope = 0.5 * (1.0 + erf_part) + upper * jnp.exp(-0.5 * upper * upper) * INV_ROOT_TWO_PI
    grad_u = times_transposed(grad_m, b_down) * slope
    grad_u_b = grad_u.astype(jnp.bfloat16)
    g_w_up = pair_sum(first_b, grad_u_b, shards)
    g_bias_up = jnp.sum(grad_u, axis=0)
    grad_y1 = grad_h2 + times_transposed(grad_u_b, b_up)
    g_gain_one = jnp.sum(grad_y1 * normed_one, axis=0)
    g_shift_one = jnp.sum(grad_y1, axis=0)
    grad_h1 = norm_back(grad_y1, normed_one, rstd_one, b_g1)
    grad_a = grad_h1.astype(jnp.bfloat16)
    g_w_out = pair_sum(ctx_flat, grad_a, shards)
    g_bias_out = jnp.sum(grad_h1, axis=0)
    grad_ctx = times_transposed(grad_a, b_out).astype(jnp.bfloat16).reshape(count, heads, HEAD_DIM)
    again = jnp.exp(scores_of(query, keys, segs) - lse)
    again_b = again.astype(jnp.bfloat16)
    delta = jnp.sum(grad_ctx.astype(jnp.float32) * ctx.astype(jnp.float32), axis=-1).T
    grad_p = jnp.einsum("qhd,khd->hqk", grad_ctx, values, preferred_element_type=jnp.float32)
    grad_s = (again * (grad_p - delta[:, :, None]) * 0.125).astype(jnp.bfloat16)
    grad_q = jnp.einsum("hqk,khd->qhd", grad_s, keys, preferred_element_type=jnp.float32).reshape(
        count, width
    )
    grad_k = jnp.einsum("hqk,qhd->khd", grad_s, query, preferred_element_type=jnp.float32).reshape(
        count, width
    )
    grad_v = jnp.einsum(
        "hqk,qhd->khd", again_b, grad_ctx, preferred_element_type=jnp.float32
    ).reshape(count, width)
    g_bias_q = jnp.sum(grad_q, axis=0)
    g_bias_v = jnp.sum(grad_v, axis=0)
    grad_qkv = jnp.concatenate([grad_q, grad_k, grad_v], axis=1).astype(jnp.bfloat16)
    g_w_qkv = pair_sum(inputs, grad_qkv, shards)
    grad_in = times_transposed(grad_qkv, b_qkv) + grad_h1
    vectors = (g_bias_q, g_bias_v, g_bias_out, g_gain_one, g_shift_one, g_bias_up, g_bias_down)
    vectors = vectors + (g_gain_two, g_shift_two)
    packed = jnp.concatenate([v.reshape(shards, -1) for v in vectors], axis=1)
    packed = scatter(packed, halving_order(shards), shards, jnp.float32).reshape(-1)
    small = []
    at = 0
    for v in vectors:
        small.append(packed[at : at + v.shape[0] // shards])
        at += v.shape[0] // shards
    return (output, grad_in, g_w_qkv, g_w_out, g_w_up, g_w_down, *small)


def solution(mesh):
    placed = (
        P("dp", None),
        P("dp", None),
        P("dp", None),
        P("dp", None),
        P("dp"),
        P("dp"),
        P("dp", None),
        P("dp"),
        P("dp"),
        P("dp"),
        P("dp", None),
        P("dp"),
        P("dp", None),
        P("dp"),
        P("dp"),
        P("dp"),
    )
    return jax.shard_map(
        functools.partial(per_device, mesh.shape["dp"]),
        mesh=mesh,
        in_specs=placed,
        out_specs=(
            P("dp", None),
            P("dp", None),
            P("dp", None),
            P("dp", None),
            P("dp", None),
            P("dp", None),
            P("dp"),
            P("dp"),
            P("dp"),
            P("dp"),
            P("dp"),
            P("dp"),
            P("dp"),
            P("dp"),
            P("dp"),
        ),
        check_vma=False,
    )
```

```python
import functools

import jax
import jax.numpy as jnp
from jax import lax
from jax.experimental import pallas as pl
from jax.experimental.pallas import tpu as pltpu
from jax.sharding import PartitionSpec as P

HEAD_DIM = 64


EPS = 1e-06
ROOT_HALF = 0.7071067811865476
INV_ROOT_TWO_PI = 0.3989422804014327
NARROW_HOPS = 2


def layer_norm(hidden, gain, shift):
    centred = hidden - jnp.mean(hidden, axis=-1, keepdims=True)
    rstd = lax.rsqrt(jnp.mean(centred * centred, axis=-1, keepdims=True) + EPS)
    normed = centred * rstd
    return (normed * gain.astype(jnp.float32) + shift.astype(jnp.float32), normed, rstd)


def norm_back(grad_y, normed, rstd, gain):
    grad_n = grad_y * gain.astype(jnp.float32)
    return rstd * (
        grad_n
        - jnp.mean(grad_n, axis=-1, keepdims=True)
        - normed * jnp.mean(grad_n * normed, axis=-1, keepdims=True)
    )


def scores_of(query, keys, segs):
    raw = jnp.einsum("qhd,khd->hqk", query, keys, preferred_element_type=jnp.float32) * 0.125
    allowed = segs[:, None] == segs[None, :]
    return jnp.where(allowed[None], raw, -1e30)


def times_transposed(left, right):
    return lax.dot_general(
        left, right, (((1,), (1,)), ((), ())), preferred_element_type=jnp.float32
    )


def transposed_times(left, right):
    return lax.dot_general(
        left, right, (((0,), (0,)), ((), ())), preferred_element_type=jnp.float32
    )


def axes_bits(shards):
    chips = shards.bit_length() - 2
    low = chips // 3
    x_bits = tuple(range(1, 1 + low))
    y_bits = tuple(range(1 + low, 1 + 2 * low))
    z_bits = tuple(range(1 + 2 * low, 1 + chips))
    return x_bits, y_bits, z_bits


def halving_order(shards, swapped=False):
    x_bits, y_bits, z_bits = axes_bits(shards)
    plane = y_bits + x_bits if swapped else x_bits + y_bits
    return (0,) + plane + z_bits


def trade(value, bit, shards):
    pairs = [(i, i ^ (1 << bit)) for i in range(shards)]
    return lax.ppermute(value, "dp", pairs)


def my_bit(bit):
    return (lax.axis_index("dp") >> bit) & 1


def scatter(value, order, shards, narrow):
    left = sorted(order, reverse=True)
    value = value.reshape((2,) * len(left) + value.shape[1:])
    for step, bit in enumerate(order):
        axis = left.index(bit)
        mine = my_bit(bit)
        keep = lax.dynamic_index_in_dim(value, mine, axis, keepdims=False)
        give = lax.dynamic_index_in_dim(value, 1 - mine, axis, keepdims=False)
        kind = jnp.bfloat16 if step < narrow else jnp.float32
        value = keep + trade(give.astype(kind), bit, shards).astype(jnp.float32)
        left.remove(bit)
    return value


def gather_kernel(shards, sizes, count, *refs):
    shard_refs, outs = refs[:count], refs[count : 2 * count]
    own_sem, send_sem, recv_sem = refs[2 * count :]
    me = lax.axis_index("dp")
    bits = shards.bit_length() - 1
    coords, starts = [], []
    low = 0
    for size in reversed(sizes):
        starts.insert(0, low)
        coords.insert(0, (me // (1 << low)) % size)
        low += size.bit_length() - 1

    def partner(bit):
        up = (me // (1 << bit)) % 2
        return me + (1 << bit) * (1 - 2 * up)

    barrier = pltpu.get_barrier_semaphore()
    for bit in range(bits):
        pl.semaphore_signal(
            barrier,
            inc=1,
            device_id=(partner(bit),),
            device_id_type=pl.DeviceIdType.MESH,
        )
    own = []
    for i in range(count):
        copy = pltpu.make_async_copy(shard_refs[i], outs[i].at[tuple(coords)], own_sem.at[i])
        copy.start()
        own.append(copy)
    pl.semaphore_wait(barrier, bits)
    for copy in own:
        copy.wait()

    def steps_of(swapped):
        steps = []
        done = []
        for axis in (0, 2, 1, 3) if swapped else (0, 1, 2, 3):
            for place in reversed(range(sizes[axis].bit_length() - 1)):
                steps.append((axis, place, tuple(done)))
            done.append(axis)
        return steps

    plans = [steps_of(False), steps_of(True)]

    def copies(i, half, step):
        axis, place, done = plans[half][step]
        span = 1 << (place + 1)
        width = outs[i].shape[-1] // 2
        made = []
        for j in range(sizes[axis] // span):
            index = [slice(None) if a in done else coords[a] for a in range(4)]
            index[axis] = j * span + coords[axis] % span
            index += [slice(None), pl.ds(half * width, width)]
            made.append(
                pltpu.make_async_remote_copy(
                    src_ref=outs[i].at[tuple(index)],
                    dst_ref=outs[i].at[tuple(index)],
                    send_sem=send_sem.at[i, half, step, j],
                    recv_sem=recv_sem.at[i, half, step, j],
                    device_id=(partner(starts[axis] + place),),
                    device_id_type=pl.DeviceIdType.MESH,
                )
            )
        return made

    live = {}
    for turn in range(count + bits):
        for i in reversed(range(count)):
            step = turn - i
            if 0 <= step <= bits:
                for half in range(2):
                    for copy in live.get((i, half, step - 1), ()):
                        copy.wait_recv()
                    if step < bits:
                        live[i, half, step] = copies(i, half, step)
                        for copy in live[i, half, step]:
                            copy.start()
    for made in live.values():
        for copy in made:
            copy.wait_send()


def gather_all(arrays, shards):
    x_bits, y_bits, z_bits = axes_bits(shards)
    sizes = (1 << len(z_bits), 1 << len(y_bits), 1 << len(x_bits), 2)
    bits = shards.bit_length() - 1
    most = max(sizes) // 2
    count = len(arrays)
    got = pl.pallas_call(
        functools.partial(gather_kernel, shards, sizes, count),
        out_shape=[jax.ShapeDtypeStruct(sizes + a.shape, a.dtype) for a in arrays],
        in_specs=[pl.BlockSpec(memory_space=pltpu.VMEM)] * count,
        out_specs=[pl.BlockSpec(memory_space=pl.ANY)] * count,
        scratch_shapes=[
            pltpu.SemaphoreType.DMA((count,)),
            pltpu.SemaphoreType.DMA((count, 2, bits, most)),
            pltpu.SemaphoreType.DMA((count, 2, bits, most)),
        ],
        compiler_params=pltpu.CompilerParams(collective_id=0, has_side_effects=True),
    )(*arrays)
    return [g.reshape(-1, a.shape[1]) for g, a in zip(got, arrays)]


def pair_sum(left, right, shards):
    tokens = left.shape[0]
    rows = left.shape[1] // shards
    split = left.reshape(tokens, shards // 2, 2, rows)
    core = my_bit(0)
    keep = lax.dynamic_index_in_dim(split, core, 2, keepdims=False).reshape(tokens, -1)
    give = lax.dynamic_index_in_dim(split, 1 - core, 2, keepdims=False).reshape(tokens, -1)
    both_left = jnp.concatenate([keep, trade(give, 0, shards)], axis=0)
    both_right = jnp.concatenate([right, trade(right, 0, shards)], axis=0)
    total = transposed_times(both_left, both_right).reshape(shards // 2, rows, -1)
    half = rows // 2
    parts = []
    for i in range(2):
        order = halving_order(shards, bool(i))[1:]
        parts.append(scatter(total[:, i * half : (i + 1) * half], order, shards, NARROW_HOPS))
    return jnp.concatenate(parts, axis=0)


def per_device(
    shards,
    inputs,
    segment_ids,
    cotangent,
    w_qkv,
    bias_q,
    bias_v,
    w_out,
    bias_out,
    gain_one,
    shift_one,
    w_up,
    bias_up,
    w_down,
    bias_down,
    gain_two,
    shift_two,
):
    count = inputs.shape[0]
    width = inputs.shape[1]
    heads = width // HEAD_DIM
    segs = segment_ids[0]
    vecs = (bias_q, bias_v, bias_out, gain_one, shift_one, bias_up, bias_down, gain_two, shift_two)
    flat = jnp.concatenate(vecs).astype(jnp.float32)
    lanes = 256
    lines = -(-flat.shape[0] // (8 * lanes)) * 8
    flat = jnp.pad(flat, (0, lines * lanes - flat.shape[0])).reshape(lines, lanes)
    every, f_qkv, f_out, f_up, f_down = gather_all((flat, w_qkv, w_out, w_up, w_down), shards)
    every = every.reshape(shards, -1)
    wide = []
    at = 0
    for v in vecs:
        wide.append(every[:, at : at + v.shape[0]].reshape(-1))
        at += v.shape[0]
    f_bq, f_bv, f_bo, f_g1, f_s1, f_bu, f_bd, f_g2, f_s2 = wide
    zeros = jnp.zeros((width,), jnp.float32)
    qkv_bias = jnp.concatenate([f_bq.astype(jnp.float32), zeros, f_bv.astype(jnp.float32)])
    qkv = (jnp.dot(inputs, f_qkv, preferred_element_type=jnp.float32) + qkv_bias).astype(
        jnp.bfloat16
    )
    query = qkv[:, :width].reshape(count, heads, HEAD_DIM)
    keys = qkv[:, width : 2 * width].reshape(count, heads, HEAD_DIM)
    values = qkv[:, 2 * width :].reshape(count, heads, HEAD_DIM)
    scores = scores_of(query, keys, segs)
    peak = jnp.max(scores, axis=-1, keepdims=True)
    lse = peak + jnp.log(jnp.sum(jnp.exp(scores - peak), axis=-1, keepdims=True))
    probs_b = jnp.exp(scores - lse).astype(jnp.bfloat16)
    ctx = jnp.einsum("hqk,khd->qhd", probs_b, values, preferred_element_type=jnp.float32).astype(
        jnp.bfloat16
    )
    ctx_flat = ctx.reshape(count, width)
    hidden_one = (
        inputs.astype(jnp.float32)
        + jnp.dot(ctx_flat, f_out, preferred_element_type=jnp.float32)
        + f_bo.astype(jnp.float32)
    )
    first, normed_one, rstd_one = layer_norm(hidden_one, f_g1, f_s1)
    first_b = first.astype(jnp.bfloat16)
    upper = jnp.dot(first_b, f_up, preferred_element_type=jnp.float32) + f_bu.astype(jnp.float32)
    erf_part = jax.scipy.special.erf(upper * ROOT_HALF)
    act = (0.5 * upper * (1.0 + erf_part)).astype(jnp.bfloat16)
    hidden_two = (
        first_b.astype(jnp.float32)
        + jnp.dot(act, f_down, preferred_element_type=jnp.float32)
        + f_bd.astype(jnp.float32)
    )
    final, normed_two, rstd_two = layer_norm(hidden_two, f_g2, f_s2)
    output = final.astype(jnp.bfloat16)
    b_qkv, b_out, b_up, b_down, b_g1, b_g2 = f_qkv, f_out, f_up, f_down, f_g1, f_g2
    grad_out = cotangent.astype(jnp.float32)
    g_gain_two = jnp.sum(grad_out * normed_two, axis=0)
    g_shift_two = jnp.sum(grad_out, axis=0)
    grad_h2 = norm_back(grad_out, normed_two, rstd_two, b_g2)
    grad_m = grad_h2.astype(jnp.bfloat16)
    g_w_down = pair_sum(act, grad_m, shards)
    g_bias_down = jnp.sum(grad_h2, axis=0)
    slope = 0.5 * (1.0 + erf_part) + upper * jnp.exp(-0.5 * upper * upper) * INV_ROOT_TWO_PI
    grad_u = times_transposed(grad_m, b_down) * slope
    grad_u_b = grad_u.astype(jnp.bfloat16)
    g_w_up = pair_sum(first_b, grad_u_b, shards)
    g_bias_up = jnp.sum(grad_u, axis=0)
    grad_y1 = grad_h2 + times_transposed(grad_u_b, b_up)
    g_gain_one = jnp.sum(grad_y1 * normed_one, axis=0)
    g_shift_one = jnp.sum(grad_y1, axis=0)
    grad_h1 = norm_back(grad_y1, normed_one, rstd_one, b_g1)
    grad_a = grad_h1.astype(jnp.bfloat16)
    g_w_out = pair_sum(ctx_flat, grad_a, shards)
    g_bias_out = jnp.sum(grad_h1, axis=0)
    grad_ctx = times_transposed(grad_a, b_out).astype(jnp.bfloat16).reshape(count, heads, HEAD_DIM)
    again = jnp.exp(scores_of(query, keys, segs) - lse)
    again_b = again.astype(jnp.bfloat16)
    delta = jnp.sum(grad_ctx.astype(jnp.float32) * ctx.astype(jnp.float32), axis=-1).T
    grad_p = jnp.einsum("qhd,khd->hqk", grad_ctx, values, preferred_element_type=jnp.float32)
    grad_s = (again * (grad_p - delta[:, :, None]) * 0.125).astype(jnp.bfloat16)
    grad_q = jnp.einsum("hqk,khd->qhd", grad_s, keys, preferred_element_type=jnp.float32).reshape(
        count, width
    )
    grad_k = jnp.einsum("hqk,qhd->khd", grad_s, query, preferred_element_type=jnp.float32).reshape(
        count, width
    )
    grad_v = jnp.einsum(
        "hqk,qhd->khd", again_b, grad_ctx, preferred_element_type=jnp.float32
    ).reshape(count, width)
    g_bias_q = jnp.sum(grad_q, axis=0)
    g_bias_v = jnp.sum(grad_v, axis=0)
    grad_qkv = jnp.concatenate([grad_q, grad_k, grad_v], axis=1).astype(jnp.bfloat16)
    g_w_qkv = pair_sum(inputs, grad_qkv, shards)
    grad_in = times_transposed(grad_qkv, b_qkv) + grad_h1
    vectors = (g_bias_q, g_bias_v, g_bias_out, g_gain_one, g_shift_one, g_bias_up, g_bias_down)
    vectors = vectors + (g_gain_two, g_shift_two)
    packed = jnp.concatenate([v.reshape(shards, -1) for v in vectors], axis=1)
    packed = scatter(packed, halving_order(shards), shards, 0).reshape(-1)
    small = []
    at = 0
    for v in vectors:
        small.append(packed[at : at + v.shape[0] // shards])
        at += v.shape[0] // shards
    return (output, grad_in, g_w_qkv, g_w_out, g_w_up, g_w_down, *small)


def solution(mesh):
    placed = (
        P("dp", None),
        P("dp", None),
        P("dp", None),
        P("dp", None),
        P("dp"),
        P("dp"),
        P("dp", None),
        P("dp"),
        P("dp"),
        P("dp"),
        P("dp", None),
        P("dp"),
        P("dp", None),
        P("dp"),
        P("dp"),
        P("dp"),
    )
    return jax.shard_map(
        functools.partial(per_device, mesh.shape["dp"]),
        mesh=mesh,
        in_specs=placed,
        out_specs=(
            P("dp", None),
            P("dp", None),
            P("dp", None),
            P("dp", None),
            P("dp", None),
            P("dp", None),
            P("dp"),
            P("dp"),
            P("dp"),
            P("dp"),
            P("dp"),
            P("dp"),
            P("dp"),
            P("dp"),
            P("dp"),
        ),
        check_vma=False,
    )
```

```python
import functools

import jax
import jax.numpy as jnp
from jax import lax
from jax.experimental import pallas as pl
from jax.experimental.pallas import tpu as pltpu
from jax.sharding import PartitionSpec as P

HEAD_DIM = 64


EPS = 1e-06
ROOT_HALF = 0.7071067811865476
INV_ROOT_TWO_PI = 0.3989422804014327
NARROW_HOPS = 2


def layer_norm(hidden, gain, shift):
    centred = hidden - jnp.mean(hidden, axis=-1, keepdims=True)
    rstd = lax.rsqrt(jnp.mean(centred * centred, axis=-1, keepdims=True) + EPS)
    normed = centred * rstd
    return (normed * gain.astype(jnp.float32) + shift.astype(jnp.float32), normed, rstd)


def norm_back(grad_y, normed, rstd, gain):
    grad_n = grad_y * gain.astype(jnp.float32)
    return rstd * (
        grad_n
        - jnp.mean(grad_n, axis=-1, keepdims=True)
        - normed * jnp.mean(grad_n * normed, axis=-1, keepdims=True)
    )


def scores_of(query, keys, segs):
    raw = jnp.einsum("qhd,khd->hqk", query, keys, preferred_element_type=jnp.float32) * 0.125
    allowed = segs[:, None] == segs[None, :]
    return jnp.where(allowed[None], raw, -1e30)


def times_transposed(left, right):
    return lax.dot_general(
        left, right, (((1,), (1,)), ((), ())), preferred_element_type=jnp.float32
    )


def transposed_times(left, right):
    return lax.dot_general(
        left, right, (((0,), (0,)), ((), ())), preferred_element_type=jnp.float32
    )


def axes_bits(shards):
    chips = shards.bit_length() - 2
    low = chips // 3
    x_bits = tuple(range(1, 1 + low))
    y_bits = tuple(range(1 + low, 1 + 2 * low))
    z_bits = tuple(range(1 + 2 * low, 1 + chips))
    return x_bits, y_bits, z_bits


def halving_order(shards, swapped=False):
    x_bits, y_bits, z_bits = axes_bits(shards)
    plane = y_bits + x_bits if swapped else x_bits + y_bits
    return (0,) + plane + z_bits


def trade(value, bit, shards):
    pairs = [(i, i ^ (1 << bit)) for i in range(shards)]
    return lax.ppermute(value, "dp", pairs)


def my_bit(bit):
    return (lax.axis_index("dp") >> bit) & 1


def scatter(value, order, shards, narrow):
    left = sorted(order, reverse=True)
    value = value.reshape((2,) * len(left) + value.shape[1:])
    for step, bit in enumerate(order):
        axis = left.index(bit)
        mine = my_bit(bit)
        keep = lax.dynamic_index_in_dim(value, mine, axis, keepdims=False)
        give = lax.dynamic_index_in_dim(value, 1 - mine, axis, keepdims=False)
        kind = jnp.bfloat16 if step < narrow else jnp.float32
        value = keep + trade(give.astype(kind), bit, shards).astype(jnp.float32)
        left.remove(bit)
    return value


def gather_kernel(shards, sizes, count, *refs):
    shard_refs, outs = refs[:count], refs[count : 2 * count]
    own_sem, send_sem, recv_sem = refs[2 * count :]
    me = lax.axis_index("dp")
    bits = shards.bit_length() - 1
    coords, starts = [], []
    low = 0
    for size in reversed(sizes):
        starts.insert(0, low)
        coords.insert(0, (me // (1 << low)) % size)
        low += size.bit_length() - 1

    def partner(bit):
        up = (me // (1 << bit)) % 2
        return me + (1 << bit) * (1 - 2 * up)

    barrier = pltpu.get_barrier_semaphore()
    for bit in range(bits):
        pl.semaphore_signal(
            barrier,
            inc=1,
            device_id=(partner(bit),),
            device_id_type=pl.DeviceIdType.MESH,
        )
    own = []
    for i in range(count):
        copy = pltpu.make_async_copy(shard_refs[i], outs[i].at[tuple(coords)], own_sem.at[i])
        copy.start()
        own.append(copy)
    pl.semaphore_wait(barrier, bits)
    for copy in own:
        copy.wait()

    def steps_of(swapped):
        steps = []
        done = []
        for axis in (0, 2, 1, 3) if swapped else (0, 1, 2, 3):
            for place in reversed(range(sizes[axis].bit_length() - 1)):
                steps.append((axis, place, tuple(done)))
            done.append(axis)
        return steps

    plans = [steps_of(False), steps_of(True)]

    def copies(i, half, step):
        axis, place, done = plans[half][step]
        span = 1 << (place + 1)
        width = outs[i].shape[-1] // 2
        made = []
        for j in range(sizes[axis] // span):
            index = [slice(None) if a in done else coords[a] for a in range(4)]
            index[axis] = j * span + coords[axis] % span
            index += [slice(None), pl.ds(half * width, width)]
            made.append(
                pltpu.make_async_remote_copy(
                    src_ref=outs[i].at[tuple(index)],
                    dst_ref=outs[i].at[tuple(index)],
                    send_sem=send_sem.at[i, half, step, j],
                    recv_sem=recv_sem.at[i, half, step, j],
                    device_id=(partner(starts[axis] + place),),
                    device_id_type=pl.DeviceIdType.MESH,
                )
            )
        return made

    live = {}
    for turn in range(count + bits):
        for i in reversed(range(count)):
            step = turn - i
            if 0 <= step <= bits:
                for half in range(2):
                    for copy in live.get((i, half, step - 1), ()):
                        copy.wait_recv()
                    if step < bits:
                        live[i, half, step] = copies(i, half, step)
                        for copy in live[i, half, step]:
                            copy.start()
    for made in live.values():
        for copy in made:
            copy.wait_send()


def gather_all(arrays, shards):
    x_bits, y_bits, z_bits = axes_bits(shards)
    sizes = (1 << len(z_bits), 1 << len(y_bits), 1 << len(x_bits), 2)
    bits = shards.bit_length() - 1
    most = max(sizes) // 2
    count = len(arrays)
    got = pl.pallas_call(
        functools.partial(gather_kernel, shards, sizes, count),
        out_shape=[jax.ShapeDtypeStruct(sizes + a.shape, a.dtype) for a in arrays],
        in_specs=[pl.BlockSpec(memory_space=pltpu.VMEM)] * count,
        out_specs=[pl.BlockSpec(memory_space=pl.ANY)] * count,
        scratch_shapes=[
            pltpu.SemaphoreType.DMA((count,)),
            pltpu.SemaphoreType.DMA((count, 2, bits, most)),
            pltpu.SemaphoreType.DMA((count, 2, bits, most)),
        ],
        compiler_params=pltpu.CompilerParams(collective_id=0, has_side_effects=True),
    )(*arrays)
    return [g.reshape(-1, a.shape[1]) for g, a in zip(got, arrays)]


def pair_sum(left, right, shards):
    tokens = left.shape[0]
    rows = left.shape[1] // shards
    split = left.reshape(tokens, shards // 2, 2, rows)
    core = my_bit(0)
    keep = lax.dynamic_index_in_dim(split, core, 2, keepdims=False).reshape(tokens, -1)
    give = lax.dynamic_index_in_dim(split, 1 - core, 2, keepdims=False).reshape(tokens, -1)
    both_left = jnp.concatenate([keep, trade(give, 0, shards)], axis=0)
    both_right = jnp.concatenate([right, trade(right, 0, shards)], axis=0)
    return transposed_times(both_left, both_right).reshape(shards // 2, rows, -1)


def owned_rows(total, shards):
    half = total.shape[1] // 2
    parts = []
    for i in range(2):
        order = halving_order(shards, bool(i))[1:]
        parts.append(scatter(total[:, i * half : (i + 1) * half], order, shards, NARROW_HOPS))
    return jnp.concatenate(parts, axis=0)


def per_device(
    shards,
    inputs,
    segment_ids,
    cotangent,
    w_qkv,
    bias_q,
    bias_v,
    w_out,
    bias_out,
    gain_one,
    shift_one,
    w_up,
    bias_up,
    w_down,
    bias_down,
    gain_two,
    shift_two,
):
    count = inputs.shape[0]
    width = inputs.shape[1]
    heads = width // HEAD_DIM
    segs = segment_ids[0]
    vecs = (bias_q, bias_v, bias_out, gain_one, shift_one, bias_up, bias_down, gain_two, shift_two)
    flat = jnp.concatenate(vecs).astype(jnp.float32)
    lanes = 256
    lines = -(-flat.shape[0] // (8 * lanes)) * 8
    flat = jnp.pad(flat, (0, lines * lanes - flat.shape[0])).reshape(lines, lanes)
    every, f_qkv, f_out, f_up, f_down = gather_all((flat, w_qkv, w_out, w_up, w_down), shards)
    every = every.reshape(shards, -1)
    wide = []
    at = 0
    for v in vecs:
        wide.append(every[:, at : at + v.shape[0]].reshape(-1))
        at += v.shape[0]
    f_bq, f_bv, f_bo, f_g1, f_s1, f_bu, f_bd, f_g2, f_s2 = wide
    zeros = jnp.zeros((width,), jnp.float32)
    qkv_bias = jnp.concatenate([f_bq.astype(jnp.float32), zeros, f_bv.astype(jnp.float32)])
    qkv = (jnp.dot(inputs, f_qkv, preferred_element_type=jnp.float32) + qkv_bias).astype(
        jnp.bfloat16
    )
    query = qkv[:, :width].reshape(count, heads, HEAD_DIM)
    keys = qkv[:, width : 2 * width].reshape(count, heads, HEAD_DIM)
    values = qkv[:, 2 * width :].reshape(count, heads, HEAD_DIM)
    scores = scores_of(query, keys, segs)
    peak = jnp.max(scores, axis=-1, keepdims=True)
    lse = peak + jnp.log(jnp.sum(jnp.exp(scores - peak), axis=-1, keepdims=True))
    probs_b = jnp.exp(scores - lse).astype(jnp.bfloat16)
    ctx = jnp.einsum("hqk,khd->qhd", probs_b, values, preferred_element_type=jnp.float32).astype(
        jnp.bfloat16
    )
    ctx_flat = ctx.reshape(count, width)
    hidden_one = (
        inputs.astype(jnp.float32)
        + jnp.dot(ctx_flat, f_out, preferred_element_type=jnp.float32)
        + f_bo.astype(jnp.float32)
    )
    first, normed_one, rstd_one = layer_norm(hidden_one, f_g1, f_s1)
    first_b = first.astype(jnp.bfloat16)
    upper = jnp.dot(first_b, f_up, preferred_element_type=jnp.float32) + f_bu.astype(jnp.float32)
    erf_part = jax.scipy.special.erf(upper * ROOT_HALF)
    act = (0.5 * upper * (1.0 + erf_part)).astype(jnp.bfloat16)
    hidden_two = (
        first_b.astype(jnp.float32)
        + jnp.dot(act, f_down, preferred_element_type=jnp.float32)
        + f_bd.astype(jnp.float32)
    )
    final, normed_two, rstd_two = layer_norm(hidden_two, f_g2, f_s2)
    output = final.astype(jnp.bfloat16)
    b_qkv, b_out, b_up, b_down, b_g1, b_g2 = f_qkv, f_out, f_up, f_down, f_g1, f_g2
    grad_out = cotangent.astype(jnp.float32)
    g_gain_two = jnp.sum(grad_out * normed_two, axis=0)
    g_shift_two = jnp.sum(grad_out, axis=0)
    grad_h2 = norm_back(grad_out, normed_two, rstd_two, b_g2)
    grad_m = grad_h2.astype(jnp.bfloat16)
    g_w_down = pair_sum(act, grad_m, shards)
    g_bias_down = jnp.sum(grad_h2, axis=0)
    slope = 0.5 * (1.0 + erf_part) + upper * jnp.exp(-0.5 * upper * upper) * INV_ROOT_TWO_PI
    grad_u = times_transposed(grad_m, b_down) * slope
    grad_u_b = grad_u.astype(jnp.bfloat16)
    grad_u_b, g_w_down = lax.optimization_barrier((grad_u_b, g_w_down))
    g_w_down = owned_rows(g_w_down, shards)
    g_w_up = pair_sum(first_b, grad_u_b, shards)
    g_bias_up = jnp.sum(grad_u, axis=0)
    grad_y1 = grad_h2 + times_transposed(grad_u_b, b_up)
    g_gain_one = jnp.sum(grad_y1 * normed_one, axis=0)
    g_shift_one = jnp.sum(grad_y1, axis=0)
    grad_h1 = norm_back(grad_y1, normed_one, rstd_one, b_g1)
    grad_a = grad_h1.astype(jnp.bfloat16)
    grad_a, g_w_up = lax.optimization_barrier((grad_a, g_w_up))
    g_w_up = owned_rows(g_w_up, shards)
    g_w_out = pair_sum(ctx_flat, grad_a, shards)
    g_bias_out = jnp.sum(grad_h1, axis=0)
    grad_ctx = times_transposed(grad_a, b_out).astype(jnp.bfloat16).reshape(count, heads, HEAD_DIM)
    again = jnp.exp(scores_of(query, keys, segs) - lse)
    again_b = again.astype(jnp.bfloat16)
    delta = jnp.sum(grad_ctx.astype(jnp.float32) * ctx.astype(jnp.float32), axis=-1).T
    grad_p = jnp.einsum("qhd,khd->hqk", grad_ctx, values, preferred_element_type=jnp.float32)
    grad_s = (again * (grad_p - delta[:, :, None]) * 0.125).astype(jnp.bfloat16)
    grad_q = jnp.einsum("hqk,khd->qhd", grad_s, keys, preferred_element_type=jnp.float32).reshape(
        count, width
    )
    grad_k = jnp.einsum("hqk,qhd->khd", grad_s, query, preferred_element_type=jnp.float32).reshape(
        count, width
    )
    grad_v = jnp.einsum(
        "hqk,qhd->khd", again_b, grad_ctx, preferred_element_type=jnp.float32
    ).reshape(count, width)
    g_bias_q = jnp.sum(grad_q, axis=0)
    g_bias_v = jnp.sum(grad_v, axis=0)
    grad_qkv = jnp.concatenate([grad_q, grad_k, grad_v], axis=1).astype(jnp.bfloat16)
    grad_qkv, g_w_out = lax.optimization_barrier((grad_qkv, g_w_out))
    g_w_out = owned_rows(g_w_out, shards)
    g_w_qkv = owned_rows(pair_sum(inputs, grad_qkv, shards), shards)
    grad_in = times_transposed(grad_qkv, b_qkv) + grad_h1
    vectors = (g_bias_q, g_bias_v, g_bias_out, g_gain_one, g_shift_one, g_bias_up, g_bias_down)
    vectors = vectors + (g_gain_two, g_shift_two)
    packed = jnp.concatenate([v.reshape(shards, -1) for v in vectors], axis=1)
    packed = scatter(packed, halving_order(shards), shards, 0).reshape(-1)
    small = []
    at = 0
    for v in vectors:
        small.append(packed[at : at + v.shape[0] // shards])
        at += v.shape[0] // shards
    return (output, grad_in, g_w_qkv, g_w_out, g_w_up, g_w_down, *small)


def solution(mesh):
    placed = (
        P("dp", None),
        P("dp", None),
        P("dp", None),
        P("dp", None),
        P("dp"),
        P("dp"),
        P("dp", None),
        P("dp"),
        P("dp"),
        P("dp"),
        P("dp", None),
        P("dp"),
        P("dp", None),
        P("dp"),
        P("dp"),
        P("dp"),
    )
    return jax.shard_map(
        functools.partial(per_device, mesh.shape["dp"]),
        mesh=mesh,
        in_specs=placed,
        out_specs=(
            P("dp", None),
            P("dp", None),
            P("dp", None),
            P("dp", None),
            P("dp", None),
            P("dp", None),
            P("dp"),
            P("dp"),
            P("dp"),
            P("dp"),
            P("dp"),
            P("dp"),
            P("dp"),
            P("dp"),
            P("dp"),
        ),
        check_vma=False,
    )
```
